32 devices in a mesh: pipe: 2 (over core), dp: 4 (over z), tensor: 4 (over y, x).
Axes of the slice: x: 2, y: 2, z: 4, core: 2. Of those that a mesh axis runs over, the one named last changes fastest.
Arguments:
- x_img: bfloat16 [2, 4, 1536, 1024], P(None, 'dp', 'tensor'), may hold values from -6 to 6
- x_txt: bfloat16 [2, 4, 1536, 154], P(None, 'dp', 'tensor'), may hold values from -6 to 6
- cond: bfloat16 [2, 4, 1536], replicated, may hold values from -6 to 6
- cot_img: bfloat16 [2, 4, 1536, 1024], P(None, 'dp', 'tensor'), may hold values from -6 to 6
- cot_txt: bfloat16 [2, 4, 1536, 154], P(None, 'dp', 'tensor'), may hold values from -6 to 6
- ada_img: bfloat16 [2, 1536, 9216], P('pipe', ('dp', 'tensor')), may hold values from -0.15625 to 0.15625
- qkv_img: bfloat16 [2, 3, 4, 384, 1536], P('pipe', None, 'tensor', 'dp'), may hold values from -0.15625 to 0.15625
- proj_img: bfloat16 [2, 4, 384, 1536], P('pipe', 'tensor', 'dp'), may hold values from -0.75 to 0.75
- fc1_img: bfloat16 [2, 1536, 6144], P('pipe', 'dp', 'tensor'), may hold values from -0.15625 to 0.15625
- fc2_img: bfloat16 [2, 1536, 6144], P('pipe', 'dp', 'tensor'), may hold values from -0.078125 to 0.078125
- ada_txt: bfloat16 [2, 1536, 9216], P('pipe', ('dp', 'tensor')), may hold values from -0.15625 to 0.15625
- qkv_txt: bfloat16 [2, 3, 4, 384, 1536], P('pipe', None, 'tensor', 'dp'), may hold values from -0.15625 to 0.15625
- proj_txt: bfloat16 [2, 4, 384, 1536], P('pipe', 'tensor', 'dp'), may hold values from -0.75 to 0.75
- fc1_txt: bfloat16 [2, 1536, 6144], P('pipe', 'dp', 'tensor'), may hold values from -0.15625 to 0.15625
- fc2_txt: bfloat16 [2, 1536, 6144], P('pipe', 'dp', 'tensor'), may hold values from -0.078125 to 0.078125
Outputs:
- section_out_img: bfloat16 [2, 2, 4, 1536, 1024], P('pipe', None, 'dp', 'tensor')
- section_out_txt: bfloat16 [2, 2, 4, 1536, 154], P('pipe', None, 'dp', 'tensor')
- section_grad_img: bfloat16 [2, 2, 4, 1536, 1024], P('pipe', None, 'dp', 'tensor')
- section_grad_txt: bfloat16 [2, 2, 4, 1536, 154], P('pipe', None, 'dp', 'tensor')
- grad_ada_img: float32 [2, 1536, 9216], P('pipe', ('dp', 'tensor'))
- grad_qkv_img: float32 [2, 3, 4, 384, 1536], P('pipe', None, 'tensor', 'dp')
- grad_proj_img: float32 [2, 4, 384, 1536], P('pipe', 'tensor', 'dp')
- grad_fc1_img: float32 [2, 1536, 6144], P('pipe', 'dp', 'tensor')
- grad_fc2_img: float32 [2, 1536, 6144], P('pipe', 'dp', 'tensor')
- grad_ada_txt: float32 [2, 1536, 9216], P('pipe', ('dp', 'tensor'))
- grad_qkv_txt: float32 [2, 3, 4, 384, 1536], P('pipe', None, 'tensor', 'dp')
- grad_proj_txt: float32 [2, 4, 384, 1536], P('pipe', 'tensor', 'dp')
- grad_fc1_txt: float32 [2, 1536, 6144], P('pipe', 'dp', 'tensor')
- grad_fc2_txt: float32 [2, 1536, 6144], P('pipe', 'dp', 'tensor')
The draws below stay inside these ranges and needn't reach their ends.
All inputs are finite; a program needn't handle non-finite values.
Results may differ from the reference program's by a relative error of at most 0.03.
Values may be sent and summed in bfloat16 or wider, within the bound.
No kernel may reach another device: no remote copies, remote signals or barrier semaphores. Data moves between devices by JAX's collectives and lax.ppermute only.
A program may use at most 640 MiB of HBM per device.

```python
from functools import partial
import jax
import jax.numpy as jnp
from jax import lax

D = 1536
HEADS = 24
HD = 64
FF = 6144
IMG = 1024
TXT = 154
MICRO = 2
SECTIONS = 2
SEQS = 4
N_TENSOR = 4


def block_levels(key, dims, shards, smallest, high):
    gain, own = 1.0, jax.random.fold_in(key, 6)
    for axis_at, shards_of in shards:
        steps = jnp.exp(jax.random.uniform(jax.random.fold_in(own, axis_at), (shards_of,), jnp.float32, smallest / len(shards), high / len(shards)))
        gain = gain * jnp.repeat(steps, dims[axis_at] // shards_of).reshape([-1 if axis == axis_at else 1 for axis in range(len(dims))])
    return gain


def noise(stream_key, dims, spread, reach, pieces=(), held_as=jnp.bfloat16):
    drawn = jax.random.normal(stream_key, dims, jnp.float32) * spread
    if len(pieces) > 0:
        drawn = block_levels(stream_key, dims, pieces, -0.22, 0.18) * drawn
    return jnp.clip(drawn, min=-reach, max=reach).astype(held_as)


def setup_inputs(seed: int = 0) -> dict:
    arg_keys = jax.random.split(jax.random.key(seed), 16)
    return {
        "x_img": noise(arg_keys[0], (MICRO, SEQS, D, IMG), 1.0, 6.0, ((1, 4), (2, 4))),
        "x_txt": noise(arg_keys[1], (MICRO, SEQS, D, TXT), 1.0, 6.0, ((1, 4), (2, 4))),
        "cond": noise(arg_keys[2], (MICRO, SEQS, D), 1.0, 6.0),
        "cot_img": noise(arg_keys[3], (MICRO, SEQS, D, IMG), 1.0, 6.0, ((1, 4), (2, 4))),
        "cot_txt": noise(arg_keys[4], (MICRO, SEQS, D, TXT), 1.0, 6.0, ((1, 4), (2, 4))),
        "ada_img": noise(arg_keys[5], (SECTIONS, D, 6 * D), D ** -0.5, 0.15625, ((0, 2), (1, 16))),
        "qkv_img": noise(arg_keys[6], (SECTIONS, 3, N_TENSOR, D // N_TENSOR, D), D ** -0.5, 0.15625, ((0, 2), (2, 4), (3, 4))),
        "proj_img": noise(arg_keys[7], (SECTIONS, N_TENSOR, D // N_TENSOR, D), HD ** -0.5, 0.75, ((0, 2), (1, 4), (2, 4))),
        "fc1_img": noise(arg_keys[8], (SECTIONS, D, FF), D ** -0.5, 0.15625, ((0, 2), (1, 4), (2, 4))),
        "fc2_img": noise(arg_keys[9], (SECTIONS, D, FF), FF ** -0.5, 0.078125, ((0, 2), (1, 4), (2, 4))),
        "ada_txt": noise(arg_keys[10], (SECTIONS, D, 6 * D), D ** -0.5, 0.15625, ((0, 2), (1, 16))),
        "qkv_txt": noise(arg_keys[11], (SECTIONS, 3, N_TENSOR, D // N_TENSOR, D), D ** -0.5, 0.15625, ((0, 2), (2, 4), (3, 4))),
        "proj_txt": noise(arg_keys[12], (SECTIONS, N_TENSOR, D // N_TENSOR, D), HD ** -0.5, 0.75, ((0, 2), (1, 4), (2, 4))),
        "fc1_txt": noise(arg_keys[13], (SECTIONS, D, FF), D ** -0.5, 0.15625, ((0, 2), (1, 4), (2, 4))),
        "fc2_txt": noise(arg_keys[14], (SECTIONS, D, FF), FF ** -0.5, 0.078125, ((0, 2), (1, 4), (2, 4))),
    }


highest = lax.Precision.HIGHEST

@jax.custom_vjp
def low(v):
    return lax.optimization_barrier(v.astype(jnp.bfloat16)).astype(jnp.float32)

@jax.custom_vjp
def low_back(v):
    return v

def low_keep(v):
    return (low(v), None)

def low_pass(kept, grad):
    return (grad,)

def back_keep(v):
    return (v, None)

def back_low(kept, grad):
    return (low(grad),)
low.defvjp(low_keep, low_pass)
low_back.defvjp(back_keep, back_low)

def layer_norm(values):
    row_mean = lax.optimization_barrier(jnp.mean(values, axis=-1, keepdims=True))
    centred = values - row_mean
    variance = lax.optimization_barrier(jnp.mean(centred * centred, axis=-1, keepdims=True))
    return centred * lax.rsqrt(variance + 1e-06)

def matmul(left, right):
    return jnp.dot(left, right, precision=highest)

def joint_block(layer_w, image_in, text_in, image_mod, text_mod):
    streams = ((image_in, image_mod, layer_w[0]), (text_in, text_mod, layer_w[1]))
    triples = []
    for inputs, mod_row, weights in streams:
        mod_parts = mod_row.reshape(6, D)
        norm_in = low(layer_norm(inputs) * (1.0 + mod_parts[1]) + mod_parts[0])
        projected = jnp.einsum('ld,cde->cle', norm_in, weights[0], precision=highest)
        triples.append(low_back(low(projected)))
    joint_qkv = jnp.concatenate(triples, axis=1).reshape(3, IMG + TXT, HEADS, HD)
    scores = jnp.einsum('qhd,khd->hqk', joint_qkv[0], joint_qkv[1], precision=highest) * HD ** (-0.5)
    scores = low_back(scores)
    attn_probs = jax.nn.softmax(scores, axis=-1)
    mixed_out = jnp.einsum('hqk,khd->qhd', low(attn_probs), joint_qkv[2], precision=highest)
    mixed_out = low_back(low(mixed_out.reshape(IMG + TXT, D)))
    results = []
    for stream, (inputs, mod_row, weights) in enumerate(streams):
        mod_parts = mod_row.reshape(6, D)
        rows_mixed = mixed_out[:IMG] if stream == 0 else mixed_out[IMG:]
        attn_out = low_back(matmul(rows_mixed, weights[1]))
        middle = inputs + mod_parts[2] * attn_out
        norm_mid = low(layer_norm(middle) * (1.0 + mod_parts[4]) + mod_parts[3])
        hidden = low_back(matmul(norm_mid, weights[2]))
        active = low(jax.nn.gelu(hidden, approximate=True))
        branch = low_back(matmul(active, weights[3]))
        results.append(middle + mod_parts[5] * branch)
    return (results[0], results[1])

def reference(x_img, x_txt, cond, cot_img, cot_txt, ada_img, qkv_img, proj_img, fc1_img, fc2_img, ada_txt, qkv_txt, proj_txt, fc1_txt, fc2_txt):
    weights = tuple((matrix.astype(jnp.float32) for matrix in (ada_img, qkv_img, proj_img, fc1_img, fc2_img, ada_txt, qkv_txt, proj_txt, fc1_txt, fc2_txt)))
    batch_rows = MICRO * SEQS
    cond_act = low(jax.nn.silu(cond.astype(jnp.float32))).reshape(batch_rows, D)

    def to_rows(values, length):
        return values.transpose(0, 1, 3, 2).reshape(batch_rows, length, D)

    def stream_weights(weights, base, section_index):
        qkv_mat = weights[base][section_index].reshape(3, D, D).transpose(0, 2, 1)
        proj_mat = weights[base + 1][section_index].reshape(D, D)
        return (qkv_mat, proj_mat, weights[base + 2][section_index], weights[base + 3][section_index].T)

    def forward(weights, image_in, text_in, image_entry, text_entry):
        current = (to_rows(image_in, IMG), to_rows(text_in, TXT))
        entries = (to_rows(image_entry, IMG), to_rows(text_entry, TXT))
        section_values = []
        for section_index in range(SECTIONS):
            if section_index > 0:
                current = (low_back(low(current[0])) + entries[0], low_back(low(current[1])) + entries[1])
            image_mod = matmul(cond_act, weights[0][section_index])
            text_mod = matmul(cond_act, weights[5][section_index])
            layer_w = (stream_weights(weights, 1, section_index), stream_weights(weights, 6, section_index))
            one_block = jax.checkpoint(partial(joint_block, layer_w))

            def scan_step(carry, items):
                return (carry, one_block(*items))
            _, current = lax.scan(scan_step, None, (current[0], current[1], image_mod, text_mod))
            section_values.append(current)
        return (current, section_values)
    zero_img = jnp.zeros((MICRO, SEQS, D, IMG), jnp.float32)
    zero_txt = jnp.zeros((MICRO, SEQS, D, TXT), jnp.float32)
    final, backward, section_values = jax.vjp(forward, weights, x_img.astype(jnp.float32), x_txt.astype(jnp.float32), zero_img, zero_txt, has_aux=True)
    cotangent = (to_rows(cot_img.astype(jnp.float32), IMG), to_rows(cot_txt.astype(jnp.float32), TXT))
    grad_weights, grad_image, grad_text, grad_image_entry, grad_text_entry = backward(cotangent)
    section_out_img = jnp.stack([values[0] for values in section_values]).reshape(SECTIONS, MICRO, SEQS, IMG, D).transpose(0, 1, 2, 4, 3).astype(jnp.bfloat16)
    section_out_txt = jnp.stack([values[1] for values in section_values]).reshape(SECTIONS, MICRO, SEQS, TXT, D).transpose(0, 1, 2, 4, 3).astype(jnp.bfloat16)
    section_grad_img = jnp.stack([grad_image, grad_image_entry]).astype(jnp.bfloat16)
    section_grad_txt = jnp.stack([grad_text, grad_text_entry]).astype(jnp.bfloat16)
    return (section_out_img, section_out_txt, section_grad_img, section_grad_txt, grad_weights[0], grad_weights[1], grad_weights[2], grad_weights[3], grad_weights[4], grad_weights[5], grad_weights[6], grad_weights[7], grad_weights[8], grad_weights[9])
```

```python
import jax
import jax.numpy as jnp
from jax import lax
from jax.sharding import PartitionSpec as P

D = 1536
HD = 64
IMG = 1024
MICRO = 2


norm_eps = 1e-06
highest = lax.Precision.HIGHEST


def as_sent(array):
    return jax.tree.map(lambda a: a.astype(jnp.bfloat16) if a.dtype == jnp.float32 else a, array)


def passed_along(array, axis, by):
    peers = lax.axis_size(axis)
    pairs = [(i, i + by) for i in range(peers) if 0 <= i + by < peers]
    return lax.ppermute(array, axis, pairs)


def row_moments(values):
    return lax.psum((values[0], values[1], values[2], values[3]), "tensor")


def widen_rows(shards):
    return jax.tree.map(
        lambda part, own: part.astype(own.dtype),
        lax.all_gather(as_sent(shards), "tensor", axis=1, tiled=True),
        shards,
    )


def narrow(terms):
    return jax.tree.map(
        lambda part: part.astype(jnp.float32),
        lax.psum_scatter(as_sent(terms), "tensor", scatter_dimension=1, tiled=True),
    )


def narrow_grads(terms):
    return jax.tree.map(
        lambda part: part.astype(jnp.float32),
        lax.psum_scatter(as_sent(terms), "tensor", scatter_dimension=1, tiled=True),
    )


def gather_dense(arrays):
    return (
        lax.all_gather(arrays[0], "dp", axis=1, tiled=True),
        lax.all_gather(arrays[1], "dp", axis=0, tiled=True),
        lax.all_gather(arrays[2], "dp", axis=0, tiled=True),
        lax.all_gather(arrays[3], "dp", axis=0, tiled=True),
        lax.all_gather(arrays[4], "dp", axis=1, tiled=True),
        lax.all_gather(arrays[5], "dp", axis=0, tiled=True),
        lax.all_gather(arrays[6], "dp", axis=0, tiled=True),
        lax.all_gather(arrays[7], "dp", axis=0, tiled=True),
    )


def shard_norm(values):
    totals = row_moments(
        (
            jnp.sum(values[0], axis=1, keepdims=True),
            jnp.sum(values[1], axis=1, keepdims=True),
            jnp.sum(values[0] * values[0], axis=1, keepdims=True),
            jnp.sum(values[1] * values[1], axis=1, keepdims=True),
        )
    )
    result = []
    for stream in range(2):
        row_mean = totals[stream] / D
        inverse = lax.rsqrt(totals[stream + 2] / D - row_mean * row_mean + norm_eps)
        result.append((row_mean, inverse))
    return tuple(result)


def apply_norm(values, stats):
    return tuple(((values[stream] - stats[stream][0]) * stats[stream][1] for stream in range(2)))


def modulate(normed, mods, shift_slot, scale_slot):
    return tuple(
        (
            (
                normed[stream] * (1.0 + mods[stream][:, scale_slot]) + mods[stream][:, shift_slot]
            ).astype(jnp.bfloat16)
            for stream in range(2)
        )
    )


def norm_back(grads_in, normed, stats, mods, scale_slot):
    scaled = tuple((grads_in[stream] * (1.0 + mods[stream][:, scale_slot]) for stream in range(2)))
    totals = row_moments(
        (
            jnp.sum(scaled[0], axis=1, keepdims=True),
            jnp.sum(scaled[1], axis=1, keepdims=True),
            jnp.sum(scaled[0] * normed[0], axis=1, keepdims=True),
            jnp.sum(scaled[1] * normed[1], axis=1, keepdims=True),
        )
    )
    return tuple(
        (
            stats[stream][1]
            * (scaled[stream] - totals[stream] / D - normed[stream] * totals[stream + 2] / D)
            for stream in range(2)
        )
    )


def gelu_back(hidden, grad):
    _, pull_back = jax.vjp(lambda value: jax.nn.gelu(value, approximate=True), hidden)
    return pull_back(grad)[0]


def split_heads(joint_qkv):
    return joint_qkv.reshape(joint_qkv.shape[:2] + (-1, HD, joint_qkv.shape[3]))


def attend(joint_qkv):
    shaped = split_heads(joint_qkv)
    inv_root = HD ** (-0.5)
    scores = (
        jnp.einsum("shdq,shdk->shqk", shaped[0], shaped[1], preferred_element_type=jnp.float32)
        * inv_root
    )
    peak_score = jnp.max(scores, axis=-1, keepdims=True)
    log_total = peak_score + jnp.log(jnp.sum(jnp.exp(scores - peak_score), axis=-1, keepdims=True))
    attn_probs = jnp.exp(scores - log_total).astype(jnp.bfloat16)
    mixed_out = jnp.einsum(
        "shqk,shdk->shdq", attn_probs, shaped[2], preferred_element_type=jnp.float32
    )
    return (mixed_out.reshape(joint_qkv.shape[1:]).astype(jnp.bfloat16), log_total)


def attend_back(joint_qkv, log_total, grad_mixed):
    shaped = split_heads(joint_qkv)
    grad_shaped = grad_mixed.reshape(grad_mixed.shape[:1] + (-1, HD, grad_mixed.shape[2]))
    inv_root = HD ** (-0.5)
    scores = (
        jnp.einsum("shdq,shdk->shqk", shaped[0], shaped[1], preferred_element_type=jnp.float32)
        * inv_root
    )
    attn_probs = jnp.exp(scores - log_total)
    grad_probs = jnp.einsum(
        "shdq,shdk->shqk", grad_shaped, shaped[2], preferred_element_type=jnp.float32
    )
    row_dot = jnp.sum(attn_probs * grad_probs, axis=-1, keepdims=True)
    grad_scores = (attn_probs * (grad_probs - row_dot)).astype(jnp.bfloat16)
    grad_query = (
        jnp.einsum("shqk,shdk->shdq", grad_scores, shaped[1], preferred_element_type=jnp.float32)
        * inv_root
    )
    grad_key = (
        jnp.einsum("shqk,shdq->shdk", grad_scores, shaped[0], preferred_element_type=jnp.float32)
        * inv_root
    )
    grad_value = jnp.einsum(
        "shqk,shdq->shdk",
        attn_probs.astype(jnp.bfloat16),
        grad_shaped,
        preferred_element_type=jnp.float32,
    )
    return (
        jnp.stack([grad_query, grad_key, grad_value]).reshape(joint_qkv.shape).astype(jnp.bfloat16)
    )


def fold_back(shards, weights, lefts, totals, row_major):
    empty = []
    for stream in range(2):
        inner_width = weights[stream].shape[1] if row_major else weights[stream].shape[0]
        empty.append(
            jnp.zeros((shards[stream].shape[0], inner_width, shards[stream].shape[2]), jnp.float32)
        )
    pieces = jax.tree.map(
        lambda part: lax.all_gather(part, "tensor", axis=1, tiled=True), as_sent(shards)
    )
    new_sums = []
    new_grads = []
    for stream in range(2):
        if row_major:
            rows = weights[stream]
            new_sums.append(
                jnp.einsum("srl,rf->sfl", pieces[stream], rows, preferred_element_type=jnp.float32)
            )
            grad_block = totals[stream]
            grad_block = grad_block + jnp.einsum(
                "sfl,srl->rf", lefts[stream], pieces[stream], preferred_element_type=jnp.float32
            )
            new_grads.append(grad_block)
        else:
            columns = weights[stream]
            new_sums.append(
                jnp.einsum(
                    "srl,er->sel", pieces[stream], columns, preferred_element_type=jnp.float32
                )
            )
            grad_block = totals[stream]
            grad_block = grad_block + jnp.einsum(
                "sel,srl->er", lefts[stream], pieces[stream], preferred_element_type=jnp.float32
            )
            new_grads.append(grad_block)
    return (tuple(new_sums), tuple(new_grads))


def local_mods(modulation, micro_index, column, local_width):
    current = lax.dynamic_index_in_dim(modulation, micro_index, 0, keepdims=False)
    result = []
    for stream in range(2):
        whole_mod = current[:, stream].reshape(current.shape[0], 6, D)
        result.append(
            lax.dynamic_slice_in_dim(whole_mod, column * local_width, local_width, 2)[..., None]
        )
    return tuple(result)


def forward_section(inputs, mods, dense_w):
    residual = tuple((value.astype(jnp.float32) for value in inputs))
    stats_in = shard_norm(residual)
    norm_in = widen_rows(modulate(apply_norm(residual, stats_in), mods, 0, 1))
    triples = tuple(
        (
            jnp.einsum(
                "sdl,ced->csel",
                norm_in[stream],
                dense_w[stream][0],
                preferred_element_type=jnp.float32,
            ).astype(jnp.bfloat16)
            for stream in range(2)
        )
    )
    joint_qkv = jnp.concatenate(triples, axis=3)
    mixed_out, log_total = attend(joint_qkv)
    split_mixed = (mixed_out[:, :, :IMG], mixed_out[:, :, IMG:])
    attn_out = narrow(
        tuple(
            (
                jnp.einsum(
                    "sel,ed->sdl",
                    split_mixed[stream],
                    dense_w[stream][1],
                    preferred_element_type=jnp.float32,
                )
                for stream in range(2)
            )
        )
    )
    middle = tuple(
        (residual[stream] + mods[stream][:, 2] * attn_out[stream] for stream in range(2))
    )
    stats_mid = shard_norm(middle)
    norm_mid = widen_rows(modulate(apply_norm(middle, stats_mid), mods, 3, 4))
    hidden = tuple(
        (
            jnp.einsum(
                "sdl,df->sfl",
                norm_mid[stream],
                dense_w[stream][2],
                preferred_element_type=jnp.float32,
            )
            for stream in range(2)
        )
    )
    active = tuple(
        (jax.nn.gelu(hidden[stream], approximate=True).astype(jnp.bfloat16) for stream in range(2))
    )
    branch = narrow(
        tuple(
            (
                jnp.einsum(
                    "sfl,df->sdl",
                    active[stream],
                    dense_w[stream][3],
                    preferred_element_type=jnp.float32,
                )
                for stream in range(2)
            )
        )
    )
    result = tuple(
        (
            (middle[stream] + mods[stream][:, 5] * branch[stream]).astype(jnp.bfloat16)
            for stream in range(2)
        )
    )
    stash_now = (
        inputs,
        attn_out,
        branch,
        stats_in,
        stats_mid,
        norm_in,
        norm_mid,
        joint_qkv,
        mixed_out,
        log_total,
        hidden,
        active,
    )
    return (result, stash_now)


def backward_section(stash_now, mods, dense_w, grad_out, grad_acc):
    (
        inputs,
        attn_out,
        branch,
        stats_in,
        stats_mid,
        norm_in,
        norm_mid,
        joint_qkv,
        mixed_out,
        log_total,
        hidden,
        active,
    ) = stash_now
    residual = tuple((value.astype(jnp.float32) for value in inputs))
    normed_in = apply_norm(residual, stats_in)
    middle = tuple(
        (residual[stream] + mods[stream][:, 2] * attn_out[stream] for stream in range(2))
    )
    normed_mid = apply_norm(middle, stats_mid)
    grad_branch = tuple(
        ((mods[stream][:, 5] * grad_out[stream]).astype(jnp.bfloat16) for stream in range(2))
    )
    gate_two = tuple((jnp.sum(grad_out[stream] * branch[stream], axis=2) for stream in range(2)))
    grad_active, fc2_grads = fold_back(
        grad_branch, (dense_w[0][3], dense_w[1][3]), active, (grad_acc[0][3], grad_acc[1][3]), True
    )
    grad_hidden = tuple(
        (gelu_back(hidden[stream], grad_active[stream]).astype(jnp.bfloat16) for stream in range(2))
    )
    fc1_grads = tuple(
        (
            grad_acc[stream][2]
            + jnp.einsum(
                "sdl,sfl->df",
                norm_mid[stream],
                grad_hidden[stream],
                preferred_element_type=jnp.float32,
            )
            for stream in range(2)
        )
    )
    grad_mid_in = narrow_grads(
        tuple(
            (
                jnp.einsum(
                    "sfl,df->sdl",
                    grad_hidden[stream],
                    dense_w[stream][2],
                    preferred_element_type=jnp.float32,
                )
                for stream in range(2)
            )
        )
    )
    shift_two = tuple((jnp.sum(grad_mid_in[stream], axis=2) for stream in range(2)))
    scale_two = tuple(
        (jnp.sum(grad_mid_in[stream] * normed_mid[stream], axis=2) for stream in range(2))
    )
    back_mid = norm_back(grad_mid_in, normed_mid, stats_mid, mods, 4)
    grad_middle = tuple((grad_out[stream] + back_mid[stream] for stream in range(2)))
    grad_attn = tuple(
        ((mods[stream][:, 2] * grad_middle[stream]).astype(jnp.bfloat16) for stream in range(2))
    )
    gate_one = tuple(
        (jnp.sum(grad_middle[stream] * attn_out[stream], axis=2) for stream in range(2))
    )
    split_mixed = (mixed_out[:, :, :IMG], mixed_out[:, :, IMG:])
    grad_split, proj_grads = fold_back(
        grad_attn,
        (dense_w[0][1], dense_w[1][1]),
        split_mixed,
        (grad_acc[0][1], grad_acc[1][1]),
        False,
    )
    grad_mixed = jnp.concatenate(grad_split, axis=2).astype(jnp.bfloat16)
    grad_joint = attend_back(joint_qkv, log_total, grad_mixed)
    grad_triples = (grad_joint[..., :IMG], grad_joint[..., IMG:])
    qkv_grads = tuple(
        (
            grad_acc[stream][0]
            + jnp.einsum(
                "sdl,csel->ced",
                norm_in[stream],
                grad_triples[stream],
                preferred_element_type=jnp.float32,
            )
            for stream in range(2)
        )
    )
    grad_in_norm = narrow_grads(
        tuple(
            (
                jnp.einsum(
                    "csel,ced->sdl",
                    grad_triples[stream],
                    dense_w[stream][0],
                    preferred_element_type=jnp.float32,
                )
                for stream in range(2)
            )
        )
    )
    shift_one = tuple((jnp.sum(grad_in_norm[stream], axis=2) for stream in range(2)))
    scale_one = tuple(
        (jnp.sum(grad_in_norm[stream] * normed_in[stream], axis=2) for stream in range(2))
    )
    back_in = norm_back(grad_in_norm, normed_in, stats_in, mods, 1)
    grad_input = tuple((grad_middle[stream] + back_in[stream] for stream in range(2)))
    mod_grads = tuple(
        (
            jnp.stack(
                [
                    shift_one[stream],
                    scale_one[stream],
                    gate_one[stream],
                    shift_two[stream],
                    scale_two[stream],
                    gate_two[stream],
                ],
                axis=1,
            )
            for stream in range(2)
        )
    )
    new_acc = tuple(
        (
            (qkv_grads[stream], proj_grads[stream], fc1_grads[stream], fc2_grads[stream])
            for stream in range(2)
        )
    )
    return (grad_input, mod_grads, new_acc)


def local(
    x_img,
    x_txt,
    cond,
    cot_img,
    cot_txt,
    ada_img,
    qkv_img,
    proj_img,
    fc1_img,
    fc2_img,
    ada_txt,
    qkv_txt,
    proj_txt,
    fc1_txt,
    fc2_txt,
):
    section_index = lax.axis_index("pipe")
    head_section = section_index == 0
    tail_section = section_index == lax.axis_size("pipe") - 1
    tick_count = MICRO + lax.axis_size("pipe") - 1
    column = lax.axis_index("tensor")
    dp_index = lax.axis_index("dp")
    seq_count = x_img.shape[1]
    local_width = x_img.shape[2]
    row_count = ada_img.shape[1]
    silu_all = jax.nn.silu(cond.astype(jnp.float32)).astype(jnp.bfloat16)
    dp_size = lax.axis_size("dp")
    row_start = (dp_index * lax.axis_size("tensor") + column) * row_count
    silu_rows = lax.dynamic_slice_in_dim(
        silu_all.reshape(-1, D), row_start, row_count, 1
    )
    partial_mods = jnp.concatenate(
        [
            jnp.dot(silu_rows, ada_img[0], preferred_element_type=jnp.float32),
            jnp.dot(silu_rows, ada_txt[0], preferred_element_type=jnp.float32),
        ],
        axis=1,
    ).reshape(MICRO, dp_size * seq_count, 12 * D)
    modulation = lax.psum(
        lax.psum_scatter(partial_mods, "dp", scatter_dimension=1, tiled=True), "tensor"
    )
    modulation = modulation.reshape(MICRO, seq_count, 2, 6 * D)
    local_w = (
        qkv_img[0, :, 0],
        proj_img[0, 0],
        fc1_img[0],
        fc2_img[0],
        qkv_txt[0, :, 0],
        proj_txt[0, 0],
        fc1_txt[0],
        fc2_txt[0],
    )
    gathered = gather_dense(local_w)
    dense_w = (gathered[:4], gathered[4:])
    received = (jnp.zeros(x_img.shape[1:], jnp.bfloat16), jnp.zeros(x_txt.shape[1:], jnp.bfloat16))
    stash_list = []
    out_list = []
    for fwd_tick in range(tick_count):
        micro_index = jnp.clip(fwd_tick - section_index, 0, MICRO - 1)
        own_slot = min(fwd_tick, MICRO - 1)
        entry = (
            jnp.where(head_section, x_img[own_slot], received[0]),
            jnp.where(head_section, x_txt[own_slot], received[1]),
        )
        mods = local_mods(modulation, micro_index, column, local_width)
        result, stash_now = forward_section(entry, mods, dense_w)
        stash_list.append((stash_now, mods, micro_index))
        out_list.append(result)
        if fwd_tick + 1 < tick_count:
            received = jax.tree.map(
                lambda part, own: part.astype(own.dtype),
                passed_along(as_sent(result), "pipe", 1),
                result,
            )
    gathered = gather_dense(local_w)
    dense_w = (gathered[:4], gathered[4:])
    grad_acc = tuple(
        (
            tuple((jnp.zeros(matrix.shape, jnp.float32) for matrix in dense_w[stream]))
            for stream in range(2)
        )
    )
    mod_grad_acc = jnp.zeros((MICRO, seq_count, 2, 6, local_width), jnp.float32)
    received = (jnp.zeros(x_img.shape[1:], jnp.bfloat16), jnp.zeros(x_txt.shape[1:], jnp.bfloat16))
    grad_list = []
    for back_turn in range(tick_count):
        fwd_tick = tick_count - 1 - back_turn
        stash_now, mods, micro_index = stash_list[fwd_tick]
        micro_raw = fwd_tick - section_index
        live_flag = ((micro_raw >= 0) & (micro_raw < MICRO)).astype(jnp.float32)
        cot_slot = min(max(MICRO - 1 - back_turn, 0), MICRO - 1)
        grad_out = (
            jnp.where(tail_section, cot_img[cot_slot], received[0]).astype(jnp.float32) * live_flag,
            jnp.where(tail_section, cot_txt[cot_slot], received[1]).astype(jnp.float32) * live_flag,
        )
        grad_input, mod_grads, grad_acc = backward_section(
            stash_now, mods, dense_w, grad_out, grad_acc
        )
        picker = (jnp.arange(MICRO) == micro_index).astype(jnp.float32)
        mod_grad_acc = (
            mod_grad_acc + picker[:, None, None, None, None] * jnp.stack(mod_grads, axis=1)[None]
        )
        grad_half = tuple((value.astype(jnp.bfloat16) for value in grad_input))
        grad_list.append(grad_half)
        if back_turn + 1 < tick_count:
            received = jax.tree.map(
                lambda part, own: part.astype(own.dtype),
                passed_along(as_sent(grad_half), "pipe", -1),
                grad_half,
            )
    flat_grads = grad_acc[0] + grad_acc[1]
    summed = (
        lax.psum_scatter(
            flat_grads[0].astype(jnp.bfloat16), "dp", scatter_dimension=1, tiled=True
        ).astype(jnp.float32),
        lax.psum_scatter(
            flat_grads[1].astype(jnp.bfloat16), "dp", scatter_dimension=0, tiled=True
        ).astype(jnp.float32),
        lax.psum_scatter(
            flat_grads[2].astype(jnp.bfloat16), "dp", scatter_dimension=0, tiled=True
        ).astype(jnp.float32),
        lax.psum_scatter(
            flat_grads[3].astype(jnp.bfloat16), "dp", scatter_dimension=0, tiled=True
        ).astype(jnp.float32),
        lax.psum_scatter(
            flat_grads[4].astype(jnp.bfloat16), "dp", scatter_dimension=1, tiled=True
        ).astype(jnp.float32),
        lax.psum_scatter(
            flat_grads[5].astype(jnp.bfloat16), "dp", scatter_dimension=0, tiled=True
        ).astype(jnp.float32),
        lax.psum_scatter(
            flat_grads[6].astype(jnp.bfloat16), "dp", scatter_dimension=0, tiled=True
        ).astype(jnp.float32),
        lax.psum_scatter(
            flat_grads[7].astype(jnp.bfloat16), "dp", scatter_dimension=0, tiled=True
        ).astype(jnp.float32),
    )
    every_mod = lax.all_gather(mod_grad_acc, ("dp", "tensor"), axis=0, tiled=False)
    every_mod = every_mod.reshape(
        (dp_size, lax.axis_size("tensor"), MICRO, seq_count, 12, local_width)
    )
    flat_mod = every_mod.transpose(2, 0, 3, 4, 1, 5).reshape(-1, 12 * D)
    ada_grad = jnp.einsum(
        "br,bf->rf", silu_rows.astype(jnp.float32), flat_mod, precision=highest
    )
    section_out_img = jnp.stack(
        [
            jnp.where(head_section, out_list[micro][0], out_list[micro + 1][0])
            for micro in range(MICRO)
        ]
    )[None]
    section_out_txt = jnp.stack(
        [
            jnp.where(head_section, out_list[micro][1], out_list[micro + 1][1])
            for micro in range(MICRO)
        ]
    )[None]
    section_grad_img = jnp.stack(
        [
            jnp.where(head_section, grad_list[MICRO - micro][0], grad_list[MICRO - 1 - micro][0])
            for micro in range(MICRO)
        ]
    )[None]
    section_grad_txt = jnp.stack(
        [
            jnp.where(head_section, grad_list[MICRO - micro][1], grad_list[MICRO - 1 - micro][1])
            for micro in range(MICRO)
        ]
    )[None]
    return (
        section_out_img,
        section_out_txt,
        section_grad_img,
        section_grad_txt,
        ada_grad[:, : 6 * D][None],
        summed[0][None, :, None],
        summed[1][None, None],
        summed[2][None],
        summed[3][None],
        ada_grad[:, 6 * D :][None],
        summed[4][None, :, None],
        summed[5][None, None],
        summed[6][None],
        summed[7][None],
    )


def solution(mesh):
    return jax.shard_map(
        local,
        mesh=mesh,
        in_specs=(
            P(None, "dp", "tensor", None),
            P(None, "dp", "tensor", None),
            P(),
            P(None, "dp", "tensor", None),
            P(None, "dp", "tensor", None),
            P("pipe", ("dp", "tensor"), None),
            P("pipe", None, "tensor", "dp", None),
            P("pipe", "tensor", "dp", None),
            P("pipe", "dp", "tensor"),
            P("pipe", "dp", "tensor"),
            P("pipe", ("dp", "tensor"), None),
            P("pipe", None, "tensor", "dp", None),
            P("pipe", "tensor", "dp", None),
            P("pipe", "dp", "tensor"),
            P("pipe", "dp", "tensor"),
        ),
        out_specs=(
            P("pipe", None, "dp", "tensor", None),
            P("pipe", None, "dp", "tensor", None),
            P("pipe", None, "dp", "tensor", None),
            P("pipe", None, "dp", "tensor", None),
            P("pipe", ("dp", "tensor"), None),
            P("pipe", None, "tensor", "dp", None),
            P("pipe", "tensor", "dp", None),
            P("pipe", "dp", "tensor"),
            P("pipe", "dp", "tensor"),
            P("pipe", ("dp", "tensor"), None),
            P("pipe", None, "tensor", "dp", None),
            P("pipe", "tensor", "dp", None),
            P("pipe", "dp", "tensor"),
            P("pipe", "dp", "tensor"),
        ),
        check_vma=False,
    )
```

```python
import jax
import jax.numpy as jnp
from jax import lax
from jax.experimental import pallas as pl
from jax.experimental.pallas import tpu as pltpu
from jax.sharding import PartitionSpec as P

D = 1536
HD = 64
MICRO = 2
TILE = 256
NORM_EPS = 1e-06
BF = jnp.bfloat16
F32 = jnp.float32
HIGHEST = lax.Precision.HIGHEST


def round_up(value, step):
    return -(-value // step) * step


def pairs(count, bit):
    return [(i, i ^ bit) for i in range(count)]


def swap_cores(array):
    return lax.ppermute(array, "pipe", pairs(2, 1))


def hop(array, bit):
    return lax.ppermute(array, "tensor", pairs(lax.axis_size("tensor"), bit))


def gather_rows(img, txt, ties=()):
    n = lax.axis_size("tensor")
    rows = img.shape[0]
    own = jnp.concatenate([img, txt], axis=0)
    if n == 4:
        half = round_up(own.shape[0] // 2, 8)
        one = hop(own, 1)
        two = hop(own, 2)
        far_a = hop(one[:half], 2)
        far_b = hop(two[half:], 1)
        far_a, far_b, ties = lax.optimization_barrier((far_a, far_b, ties))
        return (
            jnp.concatenate(
                [own[:rows], one[:rows], two[:rows], far_a, far_b[: rows - half]], axis=0
            ),
            jnp.concatenate(
                [own[rows:], one[rows:], two[rows:], far_b[rows - half :]], axis=0
            ),
        ), ties
    whole = lax.all_gather(own, "tensor", axis=0)
    return (
        whole[:, :rows].reshape(-1, own.shape[1]),
        whole[:, rows:].reshape(-1, own.shape[1]),
    ), ties


def scatter_rows(img, txt, ties=()):
    n = lax.axis_size("tensor")
    rows = img.shape[0] // n
    width = img.shape[1]
    img = img.reshape(n, rows, width)
    txt = txt.reshape(n, -1, width)
    if n == 4:
        half = round_up((rows + txt.shape[1]) // 2, 8)
        from_a = hop(img[3, :half], 1)
        from_b = hop(jnp.concatenate([img[3, half:], txt[3]], axis=0), 2)
        tail_one = jnp.concatenate([img[1, half:], txt[1]], axis=0)
        tail_one = (tail_one.astype(F32) + from_b.astype(F32)).astype(BF)
        head_two = (img[2, :half].astype(F32) + from_a.astype(F32)).astype(BF)
        one = hop(jnp.concatenate([img[1, :half], tail_one], axis=0), 1)
        two = hop(jnp.concatenate([head_two, img[2, half:], txt[2]], axis=0), 2)
        one, two, ties = lax.optimization_barrier((one, two, ties))
        return tuple(
            own.astype(F32) + a.astype(F32) + b.astype(F32)
            for own, a, b in (
                (img[0], one[:rows], two[:rows]),
                (txt[0], one[rows:], two[rows:]),
            )
        ), ties
    whole = jnp.concatenate([img, txt], axis=1)
    own = lax.psum_scatter(whole, "tensor", scatter_dimension=0, tiled=True)[0].astype(F32)
    return (own[:rows], own[rows:]), ties


def slot_ids(column):
    n = lax.axis_size("tensor")
    slots = jnp.arange(n)
    return slots ^ column if n == 4 else slots


def nt(a, b):
    return lax.dot_general(a, b, (((1,), (1,)), ((), ())), preferred_element_type=F32)


def nn(a, b):
    return lax.dot_general(a, b, (((1,), (0,)), ((), ())), preferred_element_type=F32)


def fill(scratch, first, second):
    n_first, n_second = first.shape[0], second.shape[0]
    scratch[:n_first, :] = first
    scratch[n_first : n_first + n_second, :] = second
    left = scratch.shape[0] - n_first - n_second
    if left:
        scratch[n_first + n_second :, :] = jnp.zeros((left, scratch.shape[1]), scratch.dtype)


def unit_column(rows):
    return (lax.broadcasted_iota(jnp.int32, (rows, HD), 1) == 0).astype(BF)


def attend_kernel(yi, yt, bias, oi, ot, lse, q_s, kv_s, o_s, k_s, vt_s):
    heads = yi.shape[2] // HD
    total = q_s.shape[0]
    fill(q_s, yi[0], yt[0])
    fill(kv_s, yi[1], yt[1])
    for h in range(heads):
        k_s[h] = jnp.concatenate([kv_s[:, h * HD : (h + 1) * HD], bias[...]], axis=1)
    fill(kv_s, yi[2], yt[2])
    for h in range(heads):
        vt_s[h] = jnp.transpose(kv_s[:, h * HD : (h + 1) * HD])

    @pl.loop(0, total // TILE)
    def _(step):
        rows = pl.ds(pl.multiple_of(step * TILE, TILE), TILE)
        query = q_s[rows, :] * jnp.asarray(HD**-0.5, BF)
        outs = []
        for h in range(heads):
            aug = jnp.concatenate([query[:, h * HD : (h + 1) * HD], unit_column(TILE)], axis=1)
            scores = nt(k_s[h], aug)
            peak = jnp.max(scores, axis=0, keepdims=True)
            grown = jnp.exp(scores - peak)
            mass = jnp.sum(grown, axis=0, keepdims=True)
            mixed = nn(vt_s[h], grown.astype(BF)) * (1.0 / mass)
            outs.append(jnp.transpose(mixed))
            lse[0, pl.ds(h, 1), rows] = peak + jnp.log(mass)
        o_s[rows, :] = jnp.concatenate(outs, axis=1).astype(BF)

    n_img, n_txt = oi.shape[0], ot.shape[0]
    oi[...] = o_s[:n_img, :]
    ot[...] = o_s[n_img : n_img + n_txt, :]


def attend_back_kernel(
    yi, yt, gi, gt, oi, ot, lse, bias, dyi, dyt,
    q_s, kv_s, g_s, o_s, k_s, kt_s, v_s, dq_s, dk_s, dv_s,
):
    heads = yi.shape[2] // HD
    total = q_s.shape[0]
    fill(q_s, yi[0], yt[0])
    fill(g_s, gi[...], gt[...])
    fill(o_s, oi[...], ot[...])
    fill(kv_s, yi[1], yt[1])
    for h in range(heads):
        key = kv_s[:, h * HD : (h + 1) * HD]
        k_s[h] = jnp.concatenate([key, bias[...]], axis=1)
        kt_s[h] = jnp.transpose(key)
    fill(kv_s, yi[2], yt[2])
    for h in range(heads):
        v_s[h] = kv_s[:, h * HD : (h + 1) * HD]
    dk_s[...] = jnp.zeros_like(dk_s)
    dv_s[...] = jnp.zeros_like(dv_s)

    @pl.loop(0, total // TILE)
    def _(step):
        rows = pl.ds(pl.multiple_of(step * TILE, TILE), TILE)
        query = q_s[rows, :] * jnp.asarray(HD**-0.5, BF)
        grad = g_s[rows, :]
        products = jnp.transpose(grad.astype(F32) * o_s[rows, :].astype(F32))
        outs = []
        for h in range(heads):
            part = query[:, h * HD : (h + 1) * HD]
            g_part = grad[:, h * HD : (h + 1) * HD]
            aug = jnp.concatenate([part, unit_column(TILE)], axis=1)
            probs = jnp.exp(nt(k_s[h], aug) - lse[0, pl.ds(h, 1), rows])
            row_dot = jnp.sum(products[h * HD : (h + 1) * HD, :], axis=0, keepdims=True)
            back = (probs * (nt(v_s[h], g_part) - row_dot)).astype(BF)
            dk_s[h] += nn(back, part)
            dv_s[h] += nn(probs.astype(BF), g_part)
            outs.append(jnp.transpose(nn(kt_s[h], back)))
        dq_s[rows, :] = (jnp.concatenate(outs, axis=1) * HD**-0.5).astype(BF)

    n_img, n_txt = gi.shape[0], gt.shape[0]
    dk = jnp.concatenate([dk_s[h] for h in range(heads)], axis=1).astype(BF)
    dv = jnp.concatenate([dv_s[h] for h in range(heads)], axis=1).astype(BF)
    for slot, value in ((0, dq_s[...]), (1, dk), (2, dv)):
        dyi[slot] = value[:n_img]
        dyt[slot] = value[n_img : n_img + n_txt]


def group_width(width):
    return 128 if width % 128 == 0 else width


def attend(yi, yt, bias):
    _, n_img, width = yi.shape
    n_txt = yt.shape[1]
    total = bias.shape[0]
    group = group_width(width)
    heads = group // HD
    groups = width // group
    area = groups * heads * total * total
    return pl.pallas_call(
        attend_kernel,
        grid=(groups,),
        out_shape=(
            jax.ShapeDtypeStruct((n_img, width), BF),
            jax.ShapeDtypeStruct((n_txt, width), BF),
            jax.ShapeDtypeStruct((groups, heads, total), F32),
        ),
        in_specs=[
            pl.BlockSpec((3, n_img, group), lambda g: (0, 0, g)),
            pl.BlockSpec((3, n_txt, group), lambda g: (0, 0, g)),
            pl.BlockSpec((total, HD), lambda g: (0, 0)),
        ],
        out_specs=(
            pl.BlockSpec((n_img, group), lambda g: (0, g)),
            pl.BlockSpec((n_txt, group), lambda g: (0, g)),
            pl.BlockSpec((1, heads, total), lambda g: (g, 0, 0)),
        ),
        scratch_shapes=[
            pltpu.VMEM((total, group), BF),
            pltpu.VMEM((total, group), BF),
            pltpu.VMEM((total, group), BF),
            pltpu.VMEM((heads, total, 2 * HD), BF),
            pltpu.VMEM((heads, HD, total), BF),
        ],
        compiler_params=pltpu.CompilerParams(vmem_limit_bytes=48 << 20),
        cost_estimate=pl.CostEstimate(
            flops=8 * HD * area, transcendentals=area, bytes_accessed=8 * total * width
        ),
        name="attend",
    )(yi, yt, bias)


def attend_back(yi, yt, gi, gt, oi, ot, lse, bias):
    _, n_img, width = yi.shape
    n_txt = yt.shape[1]
    total = bias.shape[0]
    group = group_width(width)
    heads = group // HD
    groups = width // group
    area = groups * heads * total * total
    triple_i = pl.BlockSpec((3, n_img, group), lambda g: (0, 0, g))
    triple_t = pl.BlockSpec((3, n_txt, group), lambda g: (0, 0, g))
    single_i = pl.BlockSpec((n_img, group), lambda g: (0, g))
    single_t = pl.BlockSpec((n_txt, group), lambda g: (0, g))
    return pl.pallas_call(
        attend_back_kernel,
        grid=(groups,),
        out_shape=(
            jax.ShapeDtypeStruct(yi.shape, BF),
            jax.ShapeDtypeStruct(yt.shape, BF),
        ),
        in_specs=[
            triple_i,
            triple_t,
            single_i,
            single_t,
            single_i,
            single_t,
            pl.BlockSpec((1, heads, total), lambda g: (g, 0, 0)),
            pl.BlockSpec((total, HD), lambda g: (0, 0)),
        ],
        out_specs=(triple_i, triple_t),
        scratch_shapes=[
            pltpu.VMEM((total, group), BF),
            pltpu.VMEM((total, group), BF),
            pltpu.VMEM((total, group), BF),
            pltpu.VMEM((total, group), BF),
            pltpu.VMEM((heads, total, 2 * HD), BF),
            pltpu.VMEM((heads, HD, total), BF),
            pltpu.VMEM((heads, total, HD), BF),
            pltpu.VMEM((total, group), BF),
            pltpu.VMEM((heads, total, HD), F32),
            pltpu.VMEM((heads, total, HD), F32),
        ],
        compiler_params=pltpu.CompilerParams(vmem_limit_bytes=48 << 20),
        cost_estimate=pl.CostEstimate(
            flops=20 * HD * area, transcendentals=area, bytes_accessed=16 * total * width
        ),
        name="attend_back",
    )(yi, yt, gi, gt, oi, ot, lse, bias)


def dot(a, b, a_dim, b_dim):
    return lax.dot_general(a, b, (((a_dim,), (b_dim,)), ((), ())), preferred_element_type=F32)


def norm_stats(values):
    mean = jnp.mean(values, axis=1, keepdims=True)
    centred = values - mean
    inverse = lax.rsqrt(jnp.mean(centred * centred, axis=1, keepdims=True) + NORM_EPS)
    return mean, inverse


def norm_back(grad, normed, inverse, scale):
    scaled = grad * (1.0 + scale)
    return inverse * (
        scaled
        - jnp.mean(scaled, axis=1, keepdims=True)
        - normed * jnp.mean(scaled * normed, axis=1, keepdims=True)
    )


def gelu(value):
    return jax.nn.gelu(value, approximate=True)


def gelu_back(hidden, grad):
    return jax.vjp(gelu, hidden)[1](grad)[0]


def each(function, *lists):
    return tuple(function(*items) for items in zip(*lists))


def pair_total(grads):
    first = lax.axis_index("pipe") == 0
    got = swap_cores(jnp.where(first, grads[1], grads[0]))
    mine = jnp.where(first, grads[0], grads[1])
    return (mine.astype(F32) + got.astype(F32)).astype(BF)


def to_owners(total, axis):
    return lax.psum_scatter(total, "dp", scatter_dimension=axis, tiled=True)


def forward_block(inputs, mods, weights, bias, grad_branch=None):
    residual = each(lambda v: v.astype(F32), inputs)
    stats_in = each(norm_stats, residual)
    normed = each(lambda v, s: (v - s[0]) * s[1], residual, stats_in)
    norm_in, _ = gather_rows(
        *each(lambda v, m: (v * (1.0 + m[1]) + m[0]).astype(BF), normed, mods)
    )
    joint = each(
        lambda v, w: jnp.einsum("td,ced->cte", v, w[0][:3], preferred_element_type=F32).astype(BF),
        norm_in,
        weights,
    )
    mixed_img, mixed_txt, lse = attend(joint[0], joint[1], bias)
    mixed = (mixed_img, mixed_txt)
    attn_out, _ = scatter_rows(*each(lambda v, w: dot(v, w[0][3], 1, 0).astype(BF), mixed, weights))
    middle = each(lambda v, a, m: v + m[2] * a, residual, attn_out, mods)
    stats_mid = each(norm_stats, middle)
    normed = each(lambda v, s: (v - s[0]) * s[1], middle, stats_mid)
    norm_mid, _ = gather_rows(
        *each(lambda v, m: (v * (1.0 + m[4]) + m[3]).astype(BF), normed, mods)
    )
    hidden = each(lambda v, w: dot(v, w[1], 1, 0), norm_mid, weights)
    active = each(lambda v: gelu(v).astype(BF), hidden)
    fc2_grad = None
    if grad_branch is not None:
        fc2_total = pair_total(
            each(lambda g, a: dot(g, a, 0, 0).astype(BF), grad_branch, active)
        )
        late = each(lambda w: w[2], weights)
        late, fc2_total = lax.optimization_barrier((late, fc2_total))
        fc2_grad = to_owners(fc2_total, 0)
        weights = each(lambda w, v: (w[0], w[1], v), weights, late)
    branch, _ = scatter_rows(*each(lambda v, w: dot(v, w[2], 1, 1).astype(BF), active, weights))
    result = each(lambda v, b, m: (v + m[5] * b).astype(BF), middle, branch, mods)
    kept = (
        inputs, stats_in, norm_in, joint, mixed, lse, attn_out, middle, stats_mid,
        norm_mid, hidden, active, branch,
    )
    return result, kept, weights, fc2_grad


def gated_branch(grad_out, mods):
    return each(lambda g, m: (m[5] * g).astype(BF), grad_out, mods)


def backward_block(
    kept, mods, weights, bias, grad_out, grad_branch, fc2_grad, beside, earlier=(None,) * 3
):
    (
        inputs, stats_in, norm_in, joint, mixed, lse, attn_out, middle, stats_mid,
        norm_mid, hidden, active, branch,
    ) = kept
    token_sum = lambda v: jnp.sum(v, axis=0)
    gate_two = each(lambda g, b: token_sum(g * b), grad_out, branch)
    fc2_total = None
    if fc2_grad is None:
        fc2_total = pair_total(
            each(lambda g, a: dot(g, a, 0, 0).astype(BF), grad_branch, active)
        )
    grad_active = each(lambda g, w: dot(g, w[2], 1, 0), grad_branch, weights)
    grad_hidden = each(lambda h, g: gelu_back(h, g).astype(BF), hidden, grad_active)
    fc1_total = pair_total(
        each(lambda v, g: dot(v, g, 0, 0).astype(BF), norm_mid, grad_hidden)
    )
    grad_norm, (fc2_total, fc1_total, done_fc2) = scatter_rows(
        *each(lambda g, w: dot(g, w[1], 1, 1).astype(BF), grad_hidden, weights),
        (fc2_total, fc1_total, earlier[2]),
    )
    if fc2_grad is None:
        fc2_grad = to_owners(fc2_total, 0)
    fc1_grad = to_owners(fc1_total, 0)
    normed = each(lambda v, s: (v - s[0]) * s[1], middle, stats_mid)
    shift_two = each(token_sum, grad_norm)
    scale_two = each(lambda g, v: token_sum(g * v), grad_norm, normed)
    grad_middle = each(
        lambda o, g, v, s, m: o + norm_back(g, v, s[1], m[4]),
        grad_out, grad_norm, normed, stats_mid, mods,
    )
    grad_attn, done_fc1 = gather_rows(
        *each(lambda g, m: (m[2] * g).astype(BF), grad_middle, mods), earlier[1]
    )
    gate_one = each(lambda g, a: token_sum(g * a), grad_middle, attn_out)
    grad_mixed = each(lambda g, w: dot(g, w[0][3], 1, 1).astype(BF), grad_attn, weights)
    proj_part = each(lambda v, g: dot(v, g, 0, 0).astype(BF), mixed, grad_attn)
    grad_joint = attend_back(*joint, *grad_mixed, *mixed, lse, bias)
    grad_joint, beside = lax.optimization_barrier((grad_joint, beside))
    qkv_part = each(
        lambda v, g: jnp.einsum("td,cte->ced", v, g, preferred_element_type=F32).astype(BF),
        norm_in,
        grad_joint,
    )
    qkvp_total = pair_total(
        each(lambda q, p: jnp.concatenate([q, p[None]], axis=0), qkv_part, proj_part)
    )
    grad_norm, (qkvp_total, done_qkvp) = scatter_rows(
        *each(
            lambda g, w: jnp.einsum(
                "cte,ced->td", g, w[0][:3], preferred_element_type=F32
            ).astype(BF),
            grad_joint,
            weights,
        ),
        (qkvp_total, earlier[0]),
    )
    qkvp_grad = to_owners(qkvp_total, 1)
    normed = each(lambda v, s: (v.astype(F32) - s[0]) * s[1], inputs, stats_in)
    shift_one = each(token_sum, grad_norm)
    scale_one = each(lambda g, v: token_sum(g * v), grad_norm, normed)
    grad_in = each(
        lambda o, g, v, s, m: (o + norm_back(g, v, s[1], m[1])).astype(BF),
        grad_middle, grad_norm, normed, stats_in, mods,
    )
    mod_grads = jnp.stack(
        [
            part[stream]
            for stream in range(2)
            for part in (shift_one, scale_one, gate_one, shift_two, scale_two, gate_two)
        ]
    )
    settled = (done_qkvp, done_fc1, done_fc2)
    return grad_in, mod_grads, (qkvp_grad, fc1_grad, fc2_grad), settled, beside


def local(
    x_img, x_txt, cond, cot_img, cot_txt,
    ada_img, qkv_img, proj_img, fc1_img, fc2_img,
    ada_txt, qkv_txt, proj_txt, fc1_txt, fc2_txt,
):
    core = lax.axis_index("pipe")
    first = core == 0
    column = lax.axis_index("tensor")
    dp_index = lax.axis_index("dp")
    n = lax.axis_size("tensor")
    dp_size = lax.axis_size("dp")
    assert lax.axis_size("pipe") == MICRO == 2 and x_img.shape[1] == 1
    feats, n_img = x_img.shape[2:]
    n_txt = x_txt.shape[3]
    img_rows = n_img // n
    txt_rows = round_up(-(-n_txt // n), 8)
    rows = img_rows + txt_rows

    def share(img, txt):
        keep = jnp.where(first, img, txt)
        got = swap_cores(jnp.where(first, txt, img))
        return jnp.where(first, keep, got), jnp.where(first, got, keep)

    shards = [
        share(
            jnp.concatenate([qkv_img[0, :, 0], proj_img[0]], axis=0),
            jnp.concatenate([qkv_txt[0, :, 0], proj_txt[0]], axis=0),
        ),
        share(fc1_img[0], fc1_txt[0]),
        share(fc2_img[0], fc2_txt[0]),
    ]
    axes = (1, 0, 0)
    weights = []
    for block in range(2):
        whole = []
        for shard, axis in zip(shards, axes):
            full = lax.all_gather(shard[block], ("pipe", "dp"), axis=axis, tiled=True)
            shape = full.shape[:axis] + (2, full.shape[axis] // 2) + full.shape[axis + 1 :]
            full = full.reshape(shape)
            whole.append([lax.index_in_dim(full, s, axis, keepdims=False) for s in range(2)])
        weights.append(tuple(tuple(item[s] for item in whole) for s in range(2)))

    def token_blocks(img, txt):
        img = lax.dynamic_index_in_dim(img[:, 0], core, 0, keepdims=False).T
        txt = lax.dynamic_index_in_dim(txt[:, 0], core, 0, keepdims=False).T
        txt = jnp.pad(txt, ((0, n * txt_rows - n_txt), (0, 0)))
        return jnp.concatenate(
            [img.reshape(n, img_rows, feats), txt.reshape(n, txt_rows, feats)], axis=1
        )

    entry = jnp.concatenate([token_blocks(x_img, x_txt), token_blocks(cot_img, cot_txt)], axis=1)
    entry = lax.all_to_all(entry, "tensor", 0, 0, tiled=True)
    entry = entry.transpose(1, 0, 2).reshape(2, rows, n * feats)
    tokens = (entry[0, :img_rows], entry[0, img_rows:])
    grad_out = (entry[1, :img_rows].astype(F32), entry[1, img_rows:].astype(F32))

    row_count = ada_img.shape[1]
    silu_all = jax.nn.silu(cond.astype(F32)).astype(BF)
    row_start = (dp_index * n + column) * row_count
    silu_rows = lax.dynamic_slice_in_dim(silu_all, row_start, row_count, 2)
    flat_rows = silu_rows.reshape(-1, row_count)
    partial_mods = jnp.stack(
        [dot(flat_rows, ada_img[0], 1, 0), dot(flat_rows, ada_txt[0], 1, 0)], axis=1
    ).reshape(MICRO, dp_size, 12, n, feats)
    partial_mods = partial_mods.transpose(1, 3, 0, 2, 4).reshape(dp_size * n, MICRO, 12, feats)
    part = lax.all_to_all(partial_mods, ("dp", "tensor"), 0, 0, tiled=True)
    part = jnp.sum(part, axis=0)
    keep = jnp.where(first, part[0], part[1])
    got = swap_cores(jnp.where(first, part[1], part[0]))
    part = jnp.stack([jnp.where(first, keep, got), jnp.where(first, got, keep)])
    mods_all = lax.all_gather(part, "tensor", axis=2, tiled=True).reshape(2, 2, 6, n * feats)
    mods = [tuple(mods_all[block, stream] for stream in range(2)) for block in range(2)]

    place = slot_ids(column)[:, None] * txt_rows + jnp.arange(txt_rows)[None]
    key_total = n_img + round_up(n * txt_rows, TILE)
    dead = jnp.concatenate(
        [
            jnp.zeros((n_img,), bool),
            (place >= n_txt).reshape(-1),
            jnp.ones((key_total - n_img - n * txt_rows,), bool),
        ]
    )
    bias = jnp.where(dead[:, None] & (jnp.arange(HD) == 0)[None], -1e30, 0.0).astype(BF)

    outs = []
    kept = []
    last_branch, _ = gather_rows(*gated_branch(grad_out, mods[1]))
    for block in range(2):
        tokens, held, weights[block], fc2_grad = forward_block(
            tokens, mods[block], weights[block], bias, last_branch if block == 1 else None
        )
        outs.append(jnp.concatenate(tokens, axis=0))
        kept.append(held)

    def to_features(blocks):
        send = jnp.stack(blocks).reshape(2, rows, n, feats).transpose(0, 2, 1, 3)
        got = lax.all_to_all(
            send.reshape(2 * n, rows, feats), ("pipe", "tensor"), 0, 0, tiled=True
        ).reshape(MICRO, n, rows, feats)
        img = got[:, :, :img_rows].transpose(0, 3, 1, 2).reshape(MICRO, feats, n_img)
        txt = got[:, :, img_rows:].transpose(0, 3, 1, 2).reshape(MICRO, feats, n * txt_rows)
        return img[None, :, None], txt[None, :, None, :, :n_txt]

    section_outs = to_features(outs)
    grads = [None, None]
    mod_grads = [None, None]
    weight_grads = [None, None]
    grad_branch = last_branch
    earlier = (None,) * 3
    for block in (1, 0):
        grad_in, mod_grads[block], weight_grads[block], settled, beside = backward_block(
            kept[block], mods[block], weights[block], bias, grad_out, grad_branch, fc2_grad,
            () if block == 1 else section_outs, earlier,
        )
        grads[block] = jnp.concatenate(grad_in, axis=0)
        if block == 1:
            grad_out = each(lambda g: g.astype(F32), grad_in)
            grad_branch, _ = gather_rows(*gated_branch(grad_out, mods[0]))
            fc2_grad = None
            earlier = weight_grads[1]
    weight_grads[1] = settled
    out_img, out_txt = beside

    grad_img, grad_txt = to_features(grads)

    keep = jnp.where(first, mod_grads[0], mod_grads[1])
    got = swap_cores(jnp.where(first, mod_grads[1], mod_grads[0]))
    both = jnp.stack([jnp.where(first, keep, got), jnp.where(first, got, keep)])
    bit = 1
    while bit < n:
        both = both + hop(both, bit)
        bit *= 2
    every = both[:, None]
    order = jnp.zeros((1,), jnp.int32)
    bit = 1
    while bit < dp_size:
        every = jnp.concatenate(
            [every, lax.ppermute(every, "dp", pairs(dp_size, bit))], axis=1
        )
        order = jnp.concatenate([order, order ^ bit])
        bit *= 2
    silu_order = jnp.take(silu_rows, order ^ dp_index, axis=1)
    ada_grads = [
        jnp.einsum(
            "mbr,mbf->rf",
            silu_order.astype(F32),
            every[:, :, 6 * s : 6 * s + 6].reshape(MICRO, dp_size, 6 * n * feats),
            precision=HIGHEST,
        )[None]
        for s in range(2)
    ]

    final = []
    for a, b in zip(*weight_grads):
        keep = jnp.where(first, a, b)
        got = jnp.where(
            first, lax.ppermute(a, "pipe", [(1, 0)]), lax.ppermute(b, "pipe", [(0, 1)])
        )
        final.append(
            (
                jnp.where(first, keep, got).astype(F32),
                jnp.where(first, got, keep).astype(F32),
            )
        )
    result = [out_img, out_txt, grad_img, grad_txt]
    for s in range(2):
        qkvp, fc1, fc2 = (item[s] for item in final)
        result += [
            ada_grads[s],
            qkvp[None, :3, None],
            qkvp[None, 3:],
            fc1[None],
            fc2[None],
        ]
    return tuple(result)


def solution(mesh):
    tokens = P(None, "dp", "tensor", None)
    ada = P("pipe", ("dp", "tensor"), None)
    qkv = P("pipe", None, "tensor", "dp", None)
    proj = P("pipe", "tensor", "dp", None)
    fc = P("pipe", "dp", "tensor")
    stream = (ada, qkv, proj, fc, fc)
    out = P("pipe", None, "dp", "tensor", None)
    return jax.shard_map(
        local,
        mesh=mesh,
        in_specs=(tokens, tokens, P(), tokens, tokens) + stream + stream,
        out_specs=(out, out, out, out) + stream + stream,
        check_vma=False,
    )
```

```python
import jax
import jax.numpy as jnp
from jax import lax
from jax.experimental import pallas as pl
from jax.experimental.pallas import tpu as pltpu
from jax.sharding import PartitionSpec as P

D = 1536
HD = 64
MICRO = 2
TILE = 256
NORM_EPS = 1e-06
BF = jnp.bfloat16
F32 = jnp.float32
HIGHEST = lax.Precision.HIGHEST


def round_up(value, step):
    return -(-value // step) * step


def pairs(count, bit):
    return [(i, i ^ bit) for i in range(count)]


def swap_cores(array):
    return lax.ppermute(array, "pipe", pairs(2, 1))


def hop(array, bit):
    return lax.ppermute(array, "tensor", pairs(lax.axis_size("tensor"), bit))


def gather_rows(img, txt, ties=()):
    n = lax.axis_size("tensor")
    rows = img.shape[0]
    own = jnp.concatenate([img, txt], axis=0)
    if n == 4:
        half = round_up(own.shape[0] // 2, 8)
        one = hop(own, 1)
        two = hop(own, 2)
        far_a = hop(one[:half], 2)
        far_b = hop(two[half:], 1)
        far_a, far_b, ties = lax.optimization_barrier((far_a, far_b, ties))
        return (
            jnp.concatenate(
                [own[:rows], one[:rows], two[:rows], far_a, far_b[: rows - half]], axis=0
            ),
            jnp.concatenate(
                [own[rows:], one[rows:], two[rows:], far_b[rows - half :]], axis=0
            ),
        ), ties
    whole = lax.all_gather(own, "tensor", axis=0)
    return (
        whole[:, :rows].reshape(-1, own.shape[1]),
        whole[:, rows:].reshape(-1, own.shape[1]),
    ), ties


def scatter_rows(img, txt, ties=()):
    n = lax.axis_size("tensor")
    rows = img.shape[0] // n
    width = img.shape[1]
    img = img.reshape(n, rows, width)
    txt = txt.reshape(n, -1, width)
    if n == 4:
        half = round_up((rows + txt.shape[1]) // 2, 8)
        from_a = hop(img[3, :half], 1)
        from_b = hop(jnp.concatenate([img[3, half:], txt[3]], axis=0), 2)
        tail_one = jnp.concatenate([img[1, half:], txt[1]], axis=0)
        tail_one = (tail_one.astype(F32) + from_b.astype(F32)).astype(BF)
        head_two = (img[2, :half].astype(F32) + from_a.astype(F32)).astype(BF)
        one = hop(jnp.concatenate([img[1, :half], tail_one], axis=0), 1)
        two = hop(jnp.concatenate([head_two, img[2, half:], txt[2]], axis=0), 2)
        one, two, ties = lax.optimization_barrier((one, two, ties))
        return tuple(
            own.astype(F32) + a.astype(F32) + b.astype(F32)
            for own, a, b in (
                (img[0], one[:rows], two[:rows]),
                (txt[0], one[rows:], two[rows:]),
            )
        ), ties
    whole = jnp.concatenate([img, txt], axis=1)
    own = lax.psum_scatter(whole, "tensor", scatter_dimension=0, tiled=True)[0].astype(F32)
    return (own[:rows], own[rows:]), ties


def slot_ids(column):
    n = lax.axis_size("tensor")
    slots = jnp.arange(n)
    return slots ^ column if n == 4 else slots


def nt(a, b):
    return lax.dot_general(a, b, (((1,), (1,)), ((), ())), preferred_element_type=F32)


def nn(a, b):
    return lax.dot_general(a, b, (((1,), (0,)), ((), ())), preferred_element_type=F32)


def fill(scratch, first, second):
    n_first, n_second = first.shape[0], second.shape[0]
    scratch[:n_first, :] = first
    scratch[n_first : n_first + n_second, :] = second
    left = scratch.shape[0] - n_first - n_second
    if left:
        scratch[n_first + n_second :, :] = jnp.zeros((left, scratch.shape[1]), scratch.dtype)


def unit_column(rows):
    return (lax.broadcasted_iota(jnp.int32, (rows, HD), 1) == 0).astype(BF)


def attend_kernel(yi, yt, bias, oi, ot, lse, q_s, kv_s, o_s, k_s, vt_s):
    heads = yi.shape[2] // HD
    total = q_s.shape[0]
    fill(q_s, yi[0], yt[0])
    fill(kv_s, yi[1], yt[1])
    for h in range(heads):
        k_s[h] = jnp.concatenate([kv_s[:, h * HD : (h + 1) * HD], bias[...]], axis=1)
    fill(kv_s, yi[2], yt[2])
    for h in range(heads):
        vt_s[h] = jnp.transpose(kv_s[:, h * HD : (h + 1) * HD])

    @pl.loop(0, total // TILE)
    def _(step):
        rows = pl.ds(pl.multiple_of(step * TILE, TILE), TILE)
        query = q_s[rows, :] * jnp.asarray(HD**-0.5, BF)
        outs = []
        for h in range(heads):
            aug = jnp.concatenate([query[:, h * HD : (h + 1) * HD], unit_column(TILE)], axis=1)
            scores = nt(k_s[h], aug)
            peak = jnp.max(scores, axis=0, keepdims=True)
            grown = jnp.exp(scores - peak)
            mass = jnp.sum(grown, axis=0, keepdims=True)
            mixed = nn(vt_s[h], grown.astype(BF)) * (1.0 / mass)
            outs.append(jnp.transpose(mixed))
            lse[0, pl.ds(h, 1), rows] = peak + jnp.log(mass)
        o_s[rows, :] = jnp.concatenate(outs, axis=1).astype(BF)

    n_img, n_txt = oi.shape[0], ot.shape[0]
    oi[...] = o_s[:n_img, :]
    ot[...] = o_s[n_img : n_img + n_txt, :]


def attend_back_kernel(
    yi, yt, gi, gt, oi, ot, lse, bias, dyi, dyt,
    q_s, kv_s, g_s, o_s, k_s, kt_s, v_s, dq_s, dk_s, dv_s,
):
    heads = yi.shape[2] // HD
    total = q_s.shape[0]
    fill(q_s, yi[0], yt[0])
    fill(g_s, gi[...], gt[...])
    fill(o_s, oi[...], ot[...])
    fill(kv_s, yi[1], yt[1])
    for h in range(heads):
        key = kv_s[:, h * HD : (h + 1) * HD]
        k_s[h] = jnp.concatenate([key, bias[...]], axis=1)
        kt_s[h] = jnp.transpose(key)
    fill(kv_s, yi[2], yt[2])
    for h in range(heads):
        v_s[h] = kv_s[:, h * HD : (h + 1) * HD]
    dk_s[...] = jnp.zeros_like(dk_s)
    dv_s[...] = jnp.zeros_like(dv_s)

    @pl.loop(0, total // TILE)
    def _(step):
        rows = pl.ds(pl.multiple_of(step * TILE, TILE), TILE)
        query = q_s[rows, :] * jnp.asarray(HD**-0.5, BF)
        grad = g_s[rows, :]
        products = jnp.transpose(grad.astype(F32) * o_s[rows, :].astype(F32))
        outs = []
        for h in range(heads):
            part = query[:, h * HD : (h + 1) * HD]
            g_part = grad[:, h * HD : (h + 1) * HD]
            aug = jnp.concatenate([part, unit_column(TILE)], axis=1)
            probs = jnp.exp(nt(k_s[h], aug) - lse[0, pl.ds(h, 1), rows])
            row_dot = jnp.sum(products[h * HD : (h + 1) * HD, :], axis=0, keepdims=True)
            back = (probs * (nt(v_s[h], g_part) - row_dot)).astype(BF)
            dk_s[h] += nn(back, part)
            dv_s[h] += nn(probs.astype(BF), g_part)
            outs.append(jnp.transpose(nn(kt_s[h], back)))
        dq_s[rows, :] = (jnp.concatenate(outs, axis=1) * HD**-0.5).astype(BF)

    n_img, n_txt = gi.shape[0], gt.shape[0]
    dk = jnp.concatenate([dk_s[h] for h in range(heads)], axis=1).astype(BF)
    dv = jnp.concatenate([dv_s[h] for h in range(heads)], axis=1).astype(BF)
    for slot, value in ((0, dq_s[...]), (1, dk), (2, dv)):
        dyi[slot] = value[:n_img]
        dyt[slot] = value[n_img : n_img + n_txt]


def group_width(width):
    return 128 if width % 128 == 0 else width


def attend(yi, yt, bias):
    _, n_img, width = yi.shape
    n_txt = yt.shape[1]
    total = bias.shape[0]
    group = group_width(width)
    heads = group // HD
    groups = width // group
    area = groups * heads * total * total
    return pl.pallas_call(
        attend_kernel,
        grid=(groups,),
        out_shape=(
            jax.ShapeDtypeStruct((n_img, width), BF),
            jax.ShapeDtypeStruct((n_txt, width), BF),
            jax.ShapeDtypeStruct((groups, heads, total), F32),
        ),
        in_specs=[
            pl.BlockSpec((3, n_img, group), lambda g: (0, 0, g)),
            pl.BlockSpec((3, n_txt, group), lambda g: (0, 0, g)),
            pl.BlockSpec((total, HD), lambda g: (0, 0)),
        ],
        out_specs=(
            pl.BlockSpec((n_img, group), lambda g: (0, g)),
            pl.BlockSpec((n_txt, group), lambda g: (0, g)),
            pl.BlockSpec((1, heads, total), lambda g: (g, 0, 0)),
        ),
        scratch_shapes=[
            pltpu.VMEM((total, group), BF),
            pltpu.VMEM((total, group), BF),
            pltpu.VMEM((total, group), BF),
            pltpu.VMEM((heads, total, 2 * HD), BF),
            pltpu.VMEM((heads, HD, total), BF),
        ],
        compiler_params=pltpu.CompilerParams(vmem_limit_bytes=48 << 20),
        cost_estimate=pl.CostEstimate(
            flops=8 * HD * area, transcendentals=area, bytes_accessed=8 * total * width
        ),
        name="attend",
    )(yi, yt, bias)


def attend_back(yi, yt, gi, gt, oi, ot, lse, bias):
    _, n_img, width = yi.shape
    n_txt = yt.shape[1]
    total = bias.shape[0]
    group = group_width(width)
    heads = group // HD
    groups = width // group
    area = groups * heads * total * total
    triple_i = pl.BlockSpec((3, n_img, group), lambda g: (0, 0, g))
    triple_t = pl.BlockSpec((3, n_txt, group), lambda g: (0, 0, g))
    single_i = pl.BlockSpec((n_img, group), lambda g: (0, g))
    single_t = pl.BlockSpec((n_txt, group), lambda g: (0, g))
    return pl.pallas_call(
        attend_back_kernel,
        grid=(groups,),
        out_shape=(
            jax.ShapeDtypeStruct(yi.shape, BF),
            jax.ShapeDtypeStruct(yt.shape, BF),
        ),
        in_specs=[
            triple_i,
            triple_t,
            single_i,
            single_t,
            single_i,
            single_t,
            pl.BlockSpec((1, heads, total), lambda g: (g, 0, 0)),
            pl.BlockSpec((total, HD), lambda g: (0, 0)),
        ],
        out_specs=(triple_i, triple_t),
        scratch_shapes=[
            pltpu.VMEM((total, group), BF),
            pltpu.VMEM((total, group), BF),
            pltpu.VMEM((total, group), BF),
            pltpu.VMEM((total, group), BF),
            pltpu.VMEM((heads, total, 2 * HD), BF),
            pltpu.VMEM((heads, HD, total), BF),
            pltpu.VMEM((heads, total, HD), BF),
            pltpu.VMEM((total, group), BF),
            pltpu.VMEM((heads, total, HD), F32),
            pltpu.VMEM((heads, total, HD), F32),
        ],
        compiler_params=pltpu.CompilerParams(vmem_limit_bytes=48 << 20),
        cost_estimate=pl.CostEstimate(
            flops=20 * HD * area, transcendentals=area, bytes_accessed=16 * total * width
        ),
        name="attend_back",
    )(yi, yt, gi, gt, oi, ot, lse, bias)


def dot(a, b, a_dim, b_dim):
    return lax.dot_general(a, b, (((a_dim,), (b_dim,)), ((), ())), preferred_element_type=F32)


def norm_stats(values):
    mean = jnp.mean(values, axis=1, keepdims=True)
    centred = values - mean
    inverse = lax.rsqrt(jnp.mean(centred * centred, axis=1, keepdims=True) + NORM_EPS)
    return mean, inverse


def norm_back(grad, normed, inverse, scale):
    scaled = grad * (1.0 + scale)
    return inverse * (
        scaled
        - jnp.mean(scaled, axis=1, keepdims=True)
        - normed * jnp.mean(scaled * normed, axis=1, keepdims=True)
    )


def gelu(value):
    return jax.nn.gelu(value, approximate=True)


def gelu_back(hidden, grad):
    return jax.vjp(gelu, hidden)[1](grad)[0]


def each(function, *lists):
    return tuple(function(*items) for items in zip(*lists))


def pair_total(grads):
    first = lax.axis_index("pipe") == 0
    got = swap_cores(jnp.where(first, grads[1], grads[0]))
    mine = jnp.where(first, grads[0], grads[1])
    return (mine.astype(F32) + got.astype(F32)).astype(BF)


def to_owners(total, axis):
    return lax.psum_scatter(total, "dp", scatter_dimension=axis, tiled=True)


def forward_block(inputs, mods, weights, bias):
    weights = by_stream(weights)
    residual = each(lambda v: v.astype(F32), inputs)
    stats_in = each(norm_stats, residual)
    normed = each(lambda v, s: (v - s[0]) * s[1], residual, stats_in)
    norm_in, _ = gather_rows(
        *each(lambda v, m: (v * (1.0 + m[1]) + m[0]).astype(BF), normed, mods)
    )
    joint = each(
        lambda v, w: jnp.einsum("td,ced->cte", v, w[0][:3], preferred_element_type=F32).astype(BF),
        norm_in,
        weights,
    )
    mixed_img, mixed_txt, lse = attend(joint[0], joint[1], bias)
    mixed = (mixed_img, mixed_txt)
    attn_out, _ = scatter_rows(*each(lambda v, w: dot(v, w[0][3], 1, 0).astype(BF), mixed, weights))
    middle = each(lambda v, a, m: v + m[2] * a, residual, attn_out, mods)
    stats_mid = each(norm_stats, middle)
    normed = each(lambda v, s: (v - s[0]) * s[1], middle, stats_mid)
    norm_mid, _ = gather_rows(
        *each(lambda v, m: (v * (1.0 + m[4]) + m[3]).astype(BF), normed, mods)
    )
    hidden = each(lambda v, w: dot(v, w[1], 1, 0), norm_mid, weights)
    active = each(lambda v: gelu(v).astype(BF), hidden)
    kept = (
        inputs, stats_in, norm_in, joint, mixed, lse, attn_out, middle, stats_mid,
        norm_mid, hidden, active,
    )
    return kept


def finish_block(active, middle, mods, weights):
    branch, _ = scatter_rows(
        *each(lambda v, w: dot(v, w[2], 1, 1).astype(BF), active, by_stream(weights))
    )
    return branch, each(lambda v, b, m: (v + m[5] * b).astype(BF), middle, branch, mods)


def by_stream(weights):
    qkvp, fc1, fc2 = weights
    return tuple((qkvp[:, s], fc1[s], fc2[s]) for s in range(2))


def gated_branch(grad_out, mods):
    return each(lambda g, m: (m[5] * g).astype(BF), grad_out, mods)


def backward_block(
    kept, mods, weights, bias, grad_out, grad_branch, fc2_grad, beside, earlier=(None,) * 3
):
    (
        inputs, stats_in, norm_in, joint, mixed, lse, attn_out, middle, stats_mid,
        norm_mid, hidden, active,
    ) = kept
    weights = by_stream(weights)
    token_sum = lambda v: jnp.sum(v, axis=0)
    grad_active = each(lambda g, w: dot(g, w[2], 1, 0), grad_branch, weights)
    grad_hidden = each(lambda h, g: gelu_back(h, g).astype(BF), hidden, grad_active)
    part = each(lambda g, w: dot(g, w[1], 1, 1).astype(BF), grad_hidden, weights)
    part, grad_hidden, held_branch = lax.optimization_barrier((part, grad_hidden, grad_branch))
    fc2_total = None
    if fc2_grad is None:
        fc2_total = pair_total(
            each(lambda g, a: dot(g, a, 0, 0).astype(BF), held_branch, active)
        )
    fc1_total = pair_total(
        each(lambda v, g: dot(v, g, 0, 0).astype(BF), norm_mid, grad_hidden)
    )
    grad_norm, (fc2_total, fc1_total, done_fc2) = scatter_rows(
        *part, (fc2_total, fc1_total, earlier[2])
    )
    if fc2_grad is None:
        fc2_grad = to_owners(fc2_total, 0)
    fc1_grad = to_owners(fc1_total, 0)
    normed = each(lambda v, s: (v - s[0]) * s[1], middle, stats_mid)
    shift_two = each(token_sum, grad_norm)
    scale_two = each(lambda g, v: token_sum(g * v), grad_norm, normed)
    grad_middle = each(
        lambda o, g, v, s, m: o + norm_back(g, v, s[1], m[4]),
        grad_out, grad_norm, normed, stats_mid, mods,
    )
    grad_attn, done_fc1 = gather_rows(
        *each(lambda g, m: (m[2] * g).astype(BF), grad_middle, mods), earlier[1]
    )
    gate_one = each(lambda g, a: token_sum(g * a), grad_middle, attn_out)
    grad_mixed = each(lambda g, w: dot(g, w[0][3], 1, 1).astype(BF), grad_attn, weights)
    grad_joint = attend_back(*joint, *grad_mixed, *mixed, lse, bias)
    part = each(
        lambda g, w: jnp.einsum(
            "cte,ced->td", g, w[0][:3], preferred_element_type=F32
        ).astype(BF),
        grad_joint,
        weights,
    )
    part, grad_joint, grad_attn, beside = lax.optimization_barrier(
        (part, grad_joint, grad_attn, beside)
    )
    proj_part = each(lambda v, g: dot(v, g, 0, 0).astype(BF), mixed, grad_attn)
    qkv_part = each(
        lambda v, g: jnp.einsum("td,cte->ced", v, g, preferred_element_type=F32).astype(BF),
        norm_in,
        grad_joint,
    )
    qkvp_total = pair_total(
        each(lambda q, p: jnp.concatenate([q, p[None]], axis=0), qkv_part, proj_part)
    )
    grad_norm, (qkvp_total, done_qkvp) = scatter_rows(*part, (qkvp_total, earlier[0]))
    qkvp_grad = to_owners(qkvp_total, 1)
    normed = each(lambda v, s: (v.astype(F32) - s[0]) * s[1], inputs, stats_in)
    shift_one = each(token_sum, grad_norm)
    scale_one = each(lambda g, v: token_sum(g * v), grad_norm, normed)
    grad_in = each(
        lambda o, g, v, s, m: (o + norm_back(g, v, s[1], m[1])).astype(BF),
        grad_middle, grad_norm, normed, stats_in, mods,
    )
    mod_grads = (shift_one, scale_one, gate_one, shift_two, scale_two)
    settled = (done_qkvp, done_fc1, done_fc2)
    return grad_in, mod_grads, (qkvp_grad, fc1_grad, fc2_grad), settled, beside


def local(
    x_img, x_txt, cond, cot_img, cot_txt,
    ada_img, qkv_img, proj_img, fc1_img, fc2_img,
    ada_txt, qkv_txt, proj_txt, fc1_txt, fc2_txt,
):
    core = lax.axis_index("pipe")
    first = core == 0
    column = lax.axis_index("tensor")
    dp_index = lax.axis_index("dp")
    n = lax.axis_size("tensor")
    dp_size = lax.axis_size("dp")
    assert lax.axis_size("pipe") == MICRO == 2 and x_img.shape[1] == 1
    feats, n_img = x_img.shape[2:]
    n_txt = x_txt.shape[3]
    img_rows = n_img // n
    txt_rows = round_up(-(-n_txt // n), 8)
    rows = img_rows + txt_rows

    def share(img, txt):
        keep = jnp.where(first, img, txt)
        got = swap_cores(jnp.where(first, txt, img))
        return jnp.where(first, keep, got), jnp.where(first, got, keep)

    shards = [
        share(
            jnp.concatenate([qkv_img[0, :, 0], proj_img[0]], axis=0),
            jnp.concatenate([qkv_txt[0, :, 0], proj_txt[0]], axis=0),
        ),
        share(fc1_img[0], fc1_txt[0]),
        share(fc2_img[0], fc2_txt[0]),
    ]
    axes = (1, 0, 0)
    weights = []
    for block in range(2):
        whole = []
        for shard, axis in zip(shards, axes):
            full = lax.all_gather(shard[block], ("pipe", "dp"), axis=axis, tiled=True)
            shape = full.shape[:axis] + (2, full.shape[axis] // 2) + full.shape[axis + 1 :]
            whole.append(full.reshape(shape))
        weights.append(tuple(whole))

    def token_blocks(img, txt):
        img = lax.dynamic_index_in_dim(img[:, 0], core, 0, keepdims=False).T
        txt = lax.dynamic_index_in_dim(txt[:, 0], core, 0, keepdims=False).T
        txt = jnp.pad(txt, ((0, n * txt_rows - n_txt), (0, 0)))
        return jnp.concatenate(
            [img.reshape(n, img_rows, feats), txt.reshape(n, txt_rows, feats)], axis=1
        )

    entry = jnp.concatenate([token_blocks(x_img, x_txt), token_blocks(cot_img, cot_txt)], axis=1)
    entry = lax.all_to_all(entry, "tensor", 0, 0, tiled=True)
    entry = entry.transpose(1, 0, 2).reshape(2, rows, n * feats)
    tokens = (entry[0, :img_rows], entry[0, img_rows:])
    grad_out = (entry[1, :img_rows].astype(F32), entry[1, img_rows:].astype(F32))

    row_count = ada_img.shape[1]
    silu_all = jax.nn.silu(cond.astype(F32)).astype(BF)
    row_start = (dp_index * n + column) * row_count
    silu_rows = lax.dynamic_slice_in_dim(silu_all, row_start, row_count, 2)
    flat_rows = silu_rows.reshape(-1, row_count)
    partial_mods = jnp.stack(
        [dot(flat_rows, ada_img[0], 1, 0), dot(flat_rows, ada_txt[0], 1, 0)], axis=1
    ).reshape(MICRO, dp_size, 12, n, feats)
    partial_mods = partial_mods.transpose(1, 3, 0, 2, 4).reshape(dp_size * n, MICRO, 12, feats)
    part = lax.all_to_all(partial_mods, ("dp", "tensor"), 0, 0, tiled=True)
    part = jnp.sum(part, axis=0)
    keep = jnp.where(first, part[0], part[1])
    got = swap_cores(jnp.where(first, part[1], part[0]))
    part = jnp.stack([jnp.where(first, keep, got), jnp.where(first, got, keep)])
    mods_all = lax.all_gather(part, "tensor", axis=2, tiled=True).reshape(2, 2, 6, n * feats)
    mods = [tuple(mods_all[block, stream] for stream in range(2)) for block in range(2)]

    place = slot_ids(column)[:, None] * txt_rows + jnp.arange(txt_rows)[None]
    key_total = n_img + round_up(n * txt_rows, TILE)
    dead = jnp.concatenate(
        [
            jnp.zeros((n_img,), bool),
            (place >= n_txt).reshape(-1),
            jnp.ones((key_total - n_img - n * txt_rows,), bool),
        ]
    )
    bias = jnp.where(dead[:, None] & (jnp.arange(HD) == 0)[None], -1e30, 0.0).astype(BF)

    def gate_sum(grad, branch):
        return each(lambda g, b: jnp.sum(g * b, axis=0), grad, branch)

    last_branch, _ = gather_rows(*gated_branch(grad_out, mods[1]))
    kept = [forward_block(tokens, mods[0], weights[0], bias)]
    branch_0, tokens = finish_block(kept[0][-1], kept[0][7], mods[0], weights[0])
    out_0 = jnp.concatenate(tokens, axis=0)
    kept.append(forward_block(tokens, mods[1], weights[1], bias))
    fc2_total = pair_total(
        each(lambda g, a: dot(g, a, 0, 0).astype(BF), last_branch, kept[1][-1])
    )
    late, fc2_total = lax.optimization_barrier((weights[1][2], fc2_total))
    weights[1] = weights[1][:2] + (late,)
    fc2_grad = to_owners(fc2_total, 0)

    def to_features(blocks):
        send = jnp.stack(blocks).reshape(2, rows, n, feats).transpose(0, 2, 1, 3)
        got = lax.all_to_all(
            send.reshape(2 * n, rows, feats), ("pipe", "tensor"), 0, 0, tiled=True
        ).reshape(MICRO, n, rows, feats)
        img = got[:, :, :img_rows].transpose(0, 3, 1, 2).reshape(MICRO, feats, n_img)
        txt = got[:, :, img_rows:].transpose(0, 3, 1, 2).reshape(MICRO, feats, n * txt_rows)
        return img[None, :, None], txt[None, :, None, :, :n_txt]

    first_in, mods_1, grads_1, _, active = backward_block(
        kept[1], mods[1], weights[1], bias, grad_out, last_branch, fc2_grad, kept[1][-1]
    )
    branch_1, last_out = finish_block(active, kept[1][7], mods[1], weights[1])
    gate_1 = gate_sum(grad_out, branch_1)
    section_outs = to_features([out_0, jnp.concatenate(last_out, axis=0)])
    grad_out = each(lambda g: g.astype(F32), first_in)
    grad_branch, _ = gather_rows(*gated_branch(grad_out, mods[0]))
    gate_0 = gate_sum(grad_out, branch_0)
    last_in, mods_0, grads_0, grads_1, (out_img, out_txt) = backward_block(
        kept[0], mods[0], weights[0], bias, grad_out, grad_branch, None, section_outs, grads_1
    )
    grads = [jnp.concatenate(last_in, axis=0), jnp.concatenate(first_in, axis=0)]
    weight_grads = [grads_0, grads_1]
    mod_grads = [
        jnp.stack([part[s] for s in range(2) for part in parts + (gate,)])
        for parts, gate in ((mods_0, gate_0), (mods_1, gate_1))
    ]

    grad_img, grad_txt = to_features(grads)

    keep = jnp.where(first, mod_grads[0], mod_grads[1])
    got = swap_cores(jnp.where(first, mod_grads[1], mod_grads[0]))
    both = jnp.stack([jnp.where(first, keep, got), jnp.where(first, got, keep)])
    bit = 1
    while bit < n:
        both = both + hop(both, bit)
        bit *= 2
    every = both[:, None].astype(BF)
    order = jnp.zeros((1,), jnp.int32)
    bit = 1
    while bit < dp_size:
        every = jnp.concatenate(
            [every, lax.ppermute(every, "dp", pairs(dp_size, bit))], axis=1
        )
        order = jnp.concatenate([order, order ^ bit])
        bit *= 2
    silu_order = jnp.take(silu_rows, order ^ dp_index, axis=1)
    ada_grads = [
        jnp.einsum(
            "mbr,mbf->rf",
            silu_order.astype(F32),
            every[:, :, 6 * s : 6 * s + 6].reshape(MICRO, dp_size, 6 * n * feats).astype(F32),
            precision=HIGHEST,
        )[None]
        for s in range(2)
    ]

    final = []
    for a, b in zip(*weight_grads):
        keep = jnp.where(first, a, b)
        got = jnp.where(
            first, lax.ppermute(a, "pipe", [(1, 0)]), lax.ppermute(b, "pipe", [(0, 1)])
        )
        final.append(
            (
                jnp.where(first, keep, got).astype(F32),
                jnp.where(first, got, keep).astype(F32),
            )
        )
    result = [out_img, out_txt, grad_img, grad_txt]
    for s in range(2):
        qkvp, fc1, fc2 = (item[s] for item in final)
        result += [
            ada_grads[s],
            qkvp[None, :3, None],
            qkvp[None, 3:],
            fc1[None],
            fc2[None],
        ]
    return tuple(result)


def solution(mesh):
    tokens = P(None, "dp", "tensor", None)
    ada = P("pipe", ("dp", "tensor"), None)
    qkv = P("pipe", None, "tensor", "dp", None)
    proj = P("pipe", "tensor", "dp", None)
    fc = P("pipe", "dp", "tensor")
    stream = (ada, qkv, proj, fc, fc)
    out = P("pipe", None, "dp", "tensor", None)
    return jax.shard_map(
        local,
        mesh=mesh,
        in_specs=(tokens, tokens, P(), tokens, tokens) + stream + stream,
        out_specs=(out, out, out, out) + stream + stream,
        check_vma=False,
    )
```
